32 devices in a mesh: groups: 2 (over y), dp: 8 (over z, x), section: 2 (over core).
Axes of the slice: x: 2, y: 2, z: 4, core: 2. Of those that a mesh axis runs over, the one named last changes fastest.
Arguments:
- boundary: bfloat16 [2, 32, 64, 8192], P('section', ('groups', 'dp')), parts along dimension 1, may hold values from -6 to 6
- w_query: bfloat16 [2, 8192, 128], P('section', 'dp'), may hold values from -8 to 8
- w_key: bfloat16 [2, 8192, 128], P('section', 'dp'), may hold values from -1 to 1
- w_value: bfloat16 [2, 8192, 128], P('section', 'dp'), may hold values from -0.0625 to 0.0625
- w_out: bfloat16 [2, 128, 8192], P('section', None, 'dp'), may hold values from -0.5 to 0.5
- norm_gain: bfloat16 [2, 8192], P('section'), may hold values from 0.099609375 to 1.8984375
- proj_wide: bfloat16 [64, 8192], replicated, may hold values from -0.0625 to 0.0625
- proj_head: bfloat16 [2, 2, 64, 128], P('section'), may hold values from -0.5 to 0.5
- lengths: int32 [32], P(('groups', 'dp')), parts along dimension 0, may hold values from 1 to 64, 614 in all
- owners: int32 [32, 1], P(('groups', 'dp')), parts along dimension 0, may hold values from 0 to 7; in each aligned block of 16 rows (0 to 15, 16 to 31, ...) at most 4 rows name the same one
Outputs:
- store: bfloat16 [64, 2, 2, 64, 64], P(('groups', 'dp'), 'section'), parts along dimension 0
The draws below stay inside these ranges and needn't reach their ends.
There are 2 independent parts, one for each index of `groups`. The reference program is written for one: setup_inputs(seed, part) draws one part's arguments, and reference() takes and returns one part's arrays. A program takes and returns all parts, laid end to end along the dimension named above; an argument that names none is the same for every part. Nothing has to cross between parts.
Inputs may be any that keep to these rules, and one draw needn't show every extreme that they name: `owners`: every owner is named by at most 4 examples, a bound that some block reaches. `lengths`: some sequence has exactly 64 tokens.
All inputs are finite; a program needn't handle non-finite values. No bound on the sum of `lengths` on one device may be relied on, other than what follows from the above.
Results may differ from the reference program's by a relative error of at most 0.013.
Values may be sent and summed in bfloat16 or wider, within the bound.
A program may use at most 128 MiB of HBM per device.

```python
import math
import jax
import jax.numpy as jnp
import numpy as np
from jax import lax

D = 8192
HD = 128
R = 64
LEN = 64
EXAMPLES = 16
CAP = 4
N_DP = 8
N_SECTION = 2


def key_matrix(key):
    return jax.random.truncated_normal(jax.random.fold_in(key, 11), -6.0, 6.0, (N_SECTION, D, HD)) * D ** (-0.5)


def draw_w_key(key, part):
    return key_matrix(key).astype(jnp.bfloat16)


def draw_w_query(key, part):
    noise = jax.random.truncated_normal(jax.random.fold_in(key, 12), -6.0, 6.0, (N_SECTION, D, HD)) * D ** (-0.5)
    return noise.astype(jnp.bfloat16)


def draw_boundary(key, part):
    first_key = jax.random.fold_in(key, 21)
    scales = jnp.array([1.0, 0.25], jnp.float32).reshape(2, 1, 1, 1)
    base = jax.random.truncated_normal(first_key, -6.0, 6.0, (2, EXAMPLES, LEN, D))
    return (base * scales).astype(jnp.bfloat16)


def steps_of(rng, shape, pieces, least, high):
    loudness, own = 1.0, jax.random.fold_in(rng, 6)
    for dim, blocks in pieces:
        steps = jnp.exp(jax.random.uniform(jax.random.fold_in(own, dim), (blocks,), jnp.float32, least / len(pieces), high / len(pieces)))
        loudness = loudness * jnp.repeat(steps, shape[dim] // blocks).reshape([-1 if axis == dim else 1 for axis in range(len(shape))])
    return loudness


def profile(number_of, total, most, skew):
    loads = [(1 << 20) // math.isqrt(rank ** skew) + 1 for rank in range(2, number_of + 1)]
    spare, given = total - most - (number_of - 1), [1] * (number_of - 1)
    while spare > 0:
        movable = [i for i in range(number_of - 1) if given[i] < most]
        pool, budget = sum([loads[i] for i in movable]), spare
        for i in movable:
            more = min(most - given[i], max(1, budget * loads[i] // pool), spare)
            given[i] = given[i] + more
            spare = spare - more
    return np.array([most] + given)


def uneven(stream_key, number_of, total, most, slope):
    if number_of == 2:
        one = jax.random.randint(stream_key, (), max(1, total - most), min(most, total - 1) + 1)
        return jnp.stack([one, total - one])
    sizes = jnp.asarray(profile(number_of, total, most, slope), jnp.int32)
    couples = (number_of - 1) // 2
    giver, receiver = sizes[1:1 + 2 * couples:2], sizes[2:2 + 2 * couples:2]
    room = jnp.minimum(giver - 1, most - receiver)
    shifted = jax.random.randint(jax.random.fold_in(stream_key, 1), (couples,), 0, 1 << 20) % (room + 1)
    sizes = sizes.at[1:1 + 2 * couples:2].set(giver - shifted).at[2:2 + 2 * couples:2].set(receiver + shifted)
    return sizes[jax.random.permutation(jax.random.fold_in(stream_key, 2), number_of)]


def routed_block(own_key, own, number, rows, number_of, top, bound, slope):
    order = jax.random.permutation(own_key, number_of)
    packed, usual = load_shares(number_of, rows * top, bound, slope, True), load_shares(number_of, rows * top, bound, slope, False)
    places = jnp.arange(number_of)

    def named(sizes, rotation):
        used = int((sizes > 0).sum())
        fixed = max(1, used // 4)
        passed = fixed + (places - fixed + rotation * (used - fixed)) % max(1, number_of - fixed)
        return jnp.zeros((number_of,), jnp.int32).at[order[jnp.where(places < fixed, places, passed)]].set(jnp.asarray(sizes, jnp.int32))

    sizes = jnp.where(number % 4 == 0, named(packed, number // 4), named(usual, number - number // 4 - 1))
    mixed = jax.random.permutation(jax.random.fold_in(own, 3), number_of)
    source_of, sink = mixed[0:number_of // 2 * 2:2], mixed[1:number_of // 2 * 2:2]
    room = jnp.minimum(sizes[source_of] - 1, bound - sizes[sink]) // 2
    room = jnp.where((source_of == order[0]) | (sink == order[0]) | (sizes[sink] == 0), 0, jnp.maximum(room, 0))
    passed = jax.random.randint(jax.random.fold_in(own, 4), (number_of // 2,), 0, 1 << 20) % (room + 1)
    sizes = sizes.at[source_of].add(-passed).at[sink].add(passed)
    members = jnp.searchsorted(jnp.cumsum(sizes), jnp.arange(rows * top), side="right").astype(jnp.int32)
    grid = members.reshape(top, rows).T
    grid = grid[jax.random.permutation(jax.random.fold_in(own, 1), rows)]
    rotation = jax.random.randint(jax.random.fold_in(own, 2), (rows, 1), 0, top)
    return jnp.take_along_axis(grid, (jnp.arange(top)[None, :] + rotation) % top, axis=1)


def load_shares(number_of, total, bound, lean, full):
    loads = [(1 << 20) // math.isqrt(rank ** lean) + 1 for rank in range(1, number_of + 1)]
    largest = bound if full else min(bound, max(-(-total // number_of), total * loads[0] // sum(loads)))
    least = 1 if total - largest >= number_of - 1 else 0
    holding, spare = [largest] + [least] * (number_of - 1), total - largest - least * (number_of - 1)
    while spare > 0:
        candidates = [i for i in range(1, number_of) if holding[i] < largest] or [i for i in range(1, number_of) if holding[i] < bound]
        mass, left = sum([loads[i] for i in candidates]), spare
        for i in candidates:
            more = min(bound - holding[i], max(1, left * loads[i] // mass), spare)
            holding[i] = holding[i] + more
            spare = spare - more
    return np.array(holding)


def centred(rng, extent, width, reach, pieces=(), dtype=jnp.bfloat16):
    gain = steps_of(rng, extent, pieces, -0.22, 0.18) if pieces else 1.0
    values = jax.random.normal(rng, extent, jnp.float32) * width * gain
    return jnp.minimum(jnp.maximum(values, -reach), reach).astype(dtype)


def setup_inputs(seed: int = 0, part: int = 0) -> dict:
    seeds = jax.random.split(jax.random.key(seed), 11)
    own_keys = jax.random.split(jax.random.fold_in(seeds[10], part), 11)
    boundary = draw_boundary(jax.random.fold_in(jax.random.fold_in(seeds[10], part), 71), part)
    w_query = draw_w_query(jax.random.fold_in(seeds[10], 71), part)
    w_key = draw_w_key(jax.random.fold_in(seeds[10], 71), part)
    w_value = centred(seeds[3], (N_SECTION, D, HD), D ** -0.5, 0.0625, ((0, 2), (1, 8)))
    w_out = centred(seeds[4], (N_SECTION, HD, D), HD ** -0.5, 0.5, ((0, 2), (2, 8)))
    norm_gain = jnp.clip(1.0 + 0.18 * jax.random.normal(seeds[5], (N_SECTION, D), jnp.float32), 0.099609375, 1.8984375).astype(jnp.bfloat16)
    proj_wide = centred(seeds[6], (R, D), D ** -0.5, 0.0625)
    proj_head = centred(seeds[7], (N_SECTION, 2, R, HD), HD ** -0.5, 0.5, ((0, 2),))
    lengths = uneven(own_keys[8], EXAMPLES, EXAMPLES * LEN * 3 // 5, LEN, 2).astype(jnp.int32)
    owners_keys = jax.random.split(jax.random.fold_in(own_keys[9], 1), EXAMPLES // EXAMPLES)
    owners_turns = jax.random.permutation(jax.random.fold_in(own_keys[9], 3), EXAMPLES // EXAMPLES)
    owners = jax.vmap(lambda own, number: routed_block(jax.random.fold_in(own_keys[9], 2), own, number, EXAMPLES, N_DP, 1, CAP, 2))(owners_keys, owners_turns).reshape((EXAMPLES, 1))
    return {"boundary": boundary, "w_query": w_query, "w_key": w_key, "w_value": w_value, "w_out": w_out, "norm_gain": norm_gain, "proj_wide": proj_wide, "proj_head": proj_head, "lengths": lengths, "owners": owners}


EPSILON = 1e-05
MASKED = -1e+30

def section_forward(hidden, zero_probe, w_query, w_key, w_value, w_out, section_gain, seq_length):
    token_count = hidden.shape[0]
    head_size = w_query.shape[1]
    widened = hidden.astype(jnp.float32)
    inverse_rms = lax.rsqrt(lax.optimization_barrier(jnp.mean(widened * widened, axis=-1, keepdims=True)) + EPSILON)
    normed = (widened * inverse_rms * section_gain.astype(jnp.float32)).astype(jnp.bfloat16)
    queries = jnp.dot(normed, w_query, preferred_element_type=jnp.float32).astype(jnp.bfloat16)
    key_vecs = jnp.dot(normed, w_key, preferred_element_type=jnp.float32).astype(jnp.bfloat16)
    values = jnp.dot(normed, w_value, preferred_element_type=jnp.float32).astype(jnp.bfloat16) + zero_probe
    scores = lax.dot_general(queries, key_vecs, (((1,), (1,)), ((), ())), preferred_element_type=jnp.float32) * head_size ** (-0.5)
    positions = jnp.arange(token_count)
    allowed = (positions[None, :] <= positions[:, None]) & (positions[None, :] < seq_length)
    scores = jnp.where(allowed, scores, MASKED)
    highest = lax.optimization_barrier(jnp.max(scores, axis=-1, keepdims=True))
    expd = jnp.exp(scores - highest)
    probs = (expd / lax.optimization_barrier(jnp.sum(expd, axis=-1, keepdims=True))).astype(jnp.bfloat16)
    mixed = jnp.dot(probs, values, preferred_element_type=jnp.float32).astype(jnp.bfloat16)
    result = (widened + jnp.dot(mixed, w_out, preferred_element_type=jnp.float32)).astype(jnp.bfloat16)
    return (result, (normed, mixed))

def module_blocks(normed, mixed, value_grad, cotangent, proj_wide, head_proj, valid):
    contract = (((1,), (1,)), ((), ()))
    across = (((0,), (0,)), ((), ()))
    valid_col = valid[:, None]
    wide_in = lax.dot_general(normed, proj_wide, contract, preferred_element_type=jnp.float32).astype(jnp.bfloat16)
    head_in = lax.dot_general(mixed, head_proj[1], contract, preferred_element_type=jnp.float32).astype(jnp.bfloat16)
    value_side = jnp.where(valid_col, lax.dot_general(value_grad, head_proj[0], contract, preferred_element_type=jnp.float32), 0.0).astype(jnp.bfloat16)
    wide_out = jnp.where(valid_col, lax.dot_general(cotangent, proj_wide, contract, preferred_element_type=jnp.float32), 0.0).astype(jnp.bfloat16)
    block_value = lax.dot_general(value_side, wide_in, across, preferred_element_type=jnp.float32)
    block_output = lax.dot_general(wide_out, head_in, across, preferred_element_type=jnp.float32)
    return jnp.stack([block_value, block_output]).astype(jnp.bfloat16)

def make_layer(w_query, w_key, w_value, w_out, section_gain, seq_length):

    def layer(hidden, zero_probe):
        return section_forward(hidden, zero_probe, w_query, w_key, w_value, w_out, section_gain, seq_length)
    return layer

def one_example(inputs, cotangent, seq_length, w_query, w_key, w_value, w_out, norm_gain, proj_wide, proj_head):
    token_count = inputs.shape[0]
    valid = jnp.arange(token_count) < seq_length
    zero_probe = jnp.zeros((token_count, w_query.shape[2]), jnp.bfloat16)
    hidden = inputs
    pullbacks = []
    extras = []
    for section_index in range(w_query.shape[0]):
        layer = make_layer(w_query[section_index], w_key[section_index], w_value[section_index], w_out[section_index], norm_gain[section_index], seq_length)
        hidden, pullback, extra = jax.vjp(layer, hidden, zero_probe, has_aux=True)
        pullbacks.append(pullback)
        extras.append(extra)
    grad_now = jnp.where(valid[:, None], cotangent, jnp.zeros_like(cotangent))
    blocks = []
    for section_index in reversed(range(w_query.shape[0])):
        hidden_grad, value_grad = pullbacks[section_index](grad_now)
        blocks.insert(0, module_blocks(extras[section_index][0], extras[section_index][1], value_grad, grad_now, proj_wide, proj_head[section_index], valid))
        grad_now = hidden_grad
    return jnp.stack(blocks)

def reference(boundary, w_query, w_key, w_value, w_out, norm_gain, proj_wide, proj_head, lengths, owners):

    def per_example(items):
        return one_example(items[0], items[1], items[2], w_query, w_key, w_value, w_out, norm_gain, proj_wide, proj_head)
    blocks = lax.map(per_example, (boundary[0], boundary[1], lengths))
    owner_ids = owners[:, 0]
    ordinal = jnp.arange(owner_ids.shape[0])
    earlier = (owner_ids[None, :] == owner_ids[:, None]) & (ordinal[None, :] < ordinal[:, None])
    slot_of = lax.optimization_barrier(jnp.sum(earlier.astype(jnp.int32), axis=1)).astype(jnp.int32)
    target_rows = (owner_ids * CAP + slot_of).astype(jnp.int32)
    store = jnp.zeros((N_DP * CAP,) + blocks.shape[1:], jnp.bfloat16)
    return store.at[target_rows].set(blocks)
```

```python
import functools

import jax
import jax.numpy as jnp
from jax import lax
from jax.experimental import pallas as pl
from jax.experimental.pallas import tpu as pltpu
from jax.sharding import PartitionSpec as P

CAP = 4
EPSILON = 1e-05
MASKED = -1e30
MESH = pl.DeviceIdType.MESH
F32 = jnp.float32
BF16 = jnp.bfloat16


def nn(a, b):
    return lax.dot_general(a, b, (((1,), (0,)), ((), ())), preferred_element_type=F32)


def nt(a, b):
    return lax.dot_general(a, b, (((1,), (1,)), ((), ())), preferred_element_type=F32)


def tn(a, b):
    return lax.dot_general(a, b, (((0,), (0,)), ((), ())), preferred_element_type=F32)


def kernel(
    n, examples, length, chunk,
    len_ref, w_ref, x_ref, gain_ref, wide_ref, head_ref, own_ref,
    out_ref,
    g_ref, wo_ref, far_ref, norm_ref, mid_ref, acc_ref, pin_ref, prb_ref,
    mix_ref, back_ref, mixin_ref, backin_ref, blk_ref, all_ref, own_all, pick_ref,
    loc_sem, send_sem, cw_sem, ccw_sem, y_sem, wo_send, wo_recv,
    x_send, x_recv, mix_send, mix_recv, back_send, back_recv,
    own_send, own_recv, blk_send, blk_recv,
):
    group = lax.axis_index("groups")
    me = lax.axis_index("dp")
    sec = lax.axis_index("section")
    rows = w_ref.shape[0]
    tokens, width = x_ref.shape
    hd = wo_ref.shape[1]
    rank = wide_ref.shape[0]
    third = rows // 3 // 16 * 16
    mid = rows - 2 * third
    mine = group * (rows - third)
    theirs = (1 - group) * (rows - third)
    half = n // 2
    parity = me % 2
    place = me // 2 + parity * (n - 1 - 2 * (me // 2))

    def at(position):
        position = (position + 2 * n) % n
        high = position // half
        return (1 - high) * 2 * position + high * (2 * (n - 1 - position) + 1)

    nxt, prv = at(place + 1), at(place - 1)

    barrier = pltpu.get_barrier_semaphore()

    def greet(i, carry):
        pl.semaphore_signal(
            barrier, inc=1, device_id={"dp": (me + i) % n}, device_id_type=MESH
        )
        return carry

    own_block = pltpu.make_async_copy(w_ref, g_ref.at[pl.ds(me * rows, rows)], loc_sem)
    own_block.start()
    lax.fori_loop(1, n, greet, 0)
    pl.semaphore_signal(barrier, inc=1, device_id={"groups": 1 - group}, device_id_type=MESH)
    pl.semaphore_signal(barrier, inc=1, device_id={"section": 1 - sec}, device_id_type=MESH)
    own_block.wait()
    pl.semaphore_wait(barrier, n + 1)

    def part(origin, offset, size):
        return g_ref.at[pl.ds(pl.multiple_of(origin * rows + offset, 16), size)]

    def hop(ref, sem, target):
        return pltpu.make_async_remote_copy(
            src_ref=ref, dst_ref=ref, send_sem=send_sem, recv_sem=sem,
            device_id=target, device_id_type=MESH,
        )

    def cw(s, origin):
        return hop(part(at(origin), mine, third), cw_sem.at[s], {"dp": nxt})

    def ccw(s, origin):
        return hop(part(at(origin), third, mid), ccw_sem.at[s], {"dp": prv})

    def over(s, origin, offset):
        return hop(part(at(origin), offset, third), y_sem.at[s], {"groups": 1 - group})

    def hand_over(origin, offset, size):
        start = pl.multiple_of(at(origin) * rows + offset, 16)

        @pl.when(sec == 0)
        def _():
            pltpu.make_async_remote_copy(
                src_ref=g_ref.at[pl.ds(start, size), pl.ds(3 * hd, hd)],
                dst_ref=wo_ref.at[pl.ds(start, size)],
                send_sem=wo_send, recv_sem=wo_recv,
                device_id={"section": 1 - sec}, device_id_type=MESH,
            ).start()

    def across(src, dst, send, recv):
        return pltpu.make_async_remote_copy(
            src_ref=src, dst_ref=dst, send_sem=send, recv_sem=recv,
            device_id={"section": 1 - sec}, device_id_type=MESH,
        )

    cw(0, place).start()
    ccw(0, place).start()
    give_x = across(x_ref, far_ref, x_send, x_recv)

    @pl.when(sec == 0)
    def _():
        give_x.start()

    hand_over(place, 0, rows)

    def tell(i, carry):
        pltpu.make_async_remote_copy(
            src_ref=own_ref, dst_ref=own_all.at[me], send_sem=own_send, recv_sem=own_recv,
            device_id={"dp": (me + i) % n}, device_id_type=MESH,
        ).start()
        return carry

    lax.fori_loop(1, n, tell, 0)
    own_all[me] = own_ref[...]

    row = lax.broadcasted_iota(jnp.int32, (tokens, 1), 0)
    reach = jnp.zeros((tokens, 1), jnp.int32)
    for e in range(examples):
        reach = jnp.where(row // length == e, len_ref[e] + e * length, reach)
    valid = row < reach
    row2 = lax.broadcasted_iota(jnp.int32, (tokens, tokens), 0)
    col2 = lax.broadcasted_iota(jnp.int32, (tokens, tokens), 1)
    allowed = (col2 <= row2) & (col2 < reach) & (row2 // length == col2 // length)
    scale = hd ** (-0.5)
    chunks = width // chunk

    def cols(c):
        return pl.ds(pl.multiple_of(c * chunk, chunk), chunk)

    def rms(ref):
        def add(c, total):
            value = ref[:, cols(c)].astype(F32)
            return total + jnp.sum(value * value, axis=1, keepdims=True)

        total = lax.fori_loop(0, chunks, add, jnp.zeros((tokens, 1), F32))
        return lax.rsqrt(total / width + EPSILON)

    def normalise(ref, inverse):
        def one(c, carry):
            value = ref[:, cols(c)].astype(F32) * inverse * gain_ref[:, cols(c)].astype(F32)
            value = value.astype(BF16)
            norm_ref[:, cols(c)] = value
            pin_ref[...] += nt(value, wide_ref[:, cols(c)])
            return carry

        lax.fori_loop(0, chunks, one, 0)

    def projections():
        acc_ref[...] = jnp.zeros_like(acc_ref)

        def one(c, carry):
            acc_ref[...] += nn(norm_ref[:, cols(c)], g_ref[cols(c), pl.ds(0, 3 * hd)])
            return carry

        lax.fori_loop(0, chunks, one, 0)

    def attention():
        q = acc_ref[:, 0:hd].astype(BF16)
        k = acc_ref[:, hd : 2 * hd].astype(BF16)
        v = acc_ref[:, 2 * hd : 3 * hd].astype(BF16)
        scores = jnp.where(allowed, nt(q, k) * scale, MASKED)
        raised = jnp.exp(scores - jnp.max(scores, axis=1, keepdims=True))
        probs = raised / jnp.sum(raised, axis=1, keepdims=True)
        mixed = nn(probs.astype(BF16), v).astype(BF16)
        return q, k, v, probs, mixed

    def finish(mixed, dvalue, wide_out):
        head_in = nt(mixed, head_ref[1]).astype(BF16)
        value_side = jnp.where(valid, nt(dvalue, head_ref[0]), 0.0).astype(BF16)
        wide_in = pin_ref[...].astype(BF16)
        for e in range(examples):
            span = slice(e * length, (e + 1) * length)
            first = tn(value_side[span], wide_in[span])
            second = tn(wide_out[span], head_in[span])
            blk_ref[e] = jnp.concatenate([first, second], axis=1).astype(BF16)

    pin_ref[...] = jnp.zeros_like(pin_ref)

    @pl.when(sec == 0)
    def _():
        normalise(x_ref, rms(x_ref))

    def step(s, carry):
        cw(s - 1, place - s).wait_recv()
        cw(s, place - s).start()
        over(s, place - s, mine).start()
        hand_over(place - s, mine, third)
        ccw(s - 1, place + s).wait_recv()
        ccw(s, place + s).start()
        hand_over(place + s, third, mid)
        return carry

    lax.fori_loop(1, n - 1, step, 0)
    cw(n - 2, place - (n - 1)).wait_recv()
    over(n - 1, place - (n - 1), mine).start()
    hand_over(place - (n - 1), mine, third)
    ccw(n - 2, place + n - 1).wait_recv()
    hand_over(place + n - 1, third, mid)

    def take(s, carry):
        over(s, place - s, theirs).wait_recv()
        hand_over(place - s, theirs, third)
        return carry

    lax.fori_loop(1, n, take, 0)

    give_mix = across(mix_ref, mixin_ref, mix_send, mix_recv)
    give_back = across(back_ref, backin_ref, back_send, back_recv)
    give_wo = across(wo_ref, wo_ref, wo_send, wo_recv)

    @pl.when(sec == 0)
    def _():
        projections()
        _, _, _, probs, mixed = attention()
        mix_ref[...] = mixed
        give_mix.start()
        prb_ref[...] = probs.astype(BF16)
        give_back.wait_recv()
        dmixed = backin_ref[:, 0:hd]
        wide_out = backin_ref[:, hd : hd + rank]
        dvalue = tn(prb_ref[...], dmixed).astype(BF16)
        finish(mix_ref[...], dvalue, wide_out)
        give_mix.wait_send()
        give_x.wait_send()
        give_wo.wait_send()

    @pl.when(sec == 1)
    def _():
        acc_ref[...] = jnp.zeros_like(acc_ref)

        def early(c, carry):
            cot = jnp.where(valid, x_ref[:, cols(c)].astype(F32), 0.0).astype(BF16)
            acc_ref[:, 0:hd] += nn(cot, g_ref[cols(c), pl.ds(3 * hd, hd)])
            acc_ref[:, hd : hd + rank] += nt(cot, wide_ref[:, cols(c)])
            return carry

        lax.fori_loop(0, chunks, early, 0)
        dmixed = acc_ref[:, 0:hd].astype(BF16)
        wide_out = acc_ref[:, hd : hd + rank].astype(BF16)
        give_x.wait_recv()
        give_wo.wait_recv()
        give_mix.wait_recv()
        before = mixin_ref[...]

        def advance(c, total):
            value = far_ref[:, cols(c)].astype(F32) + nt(before, wo_ref[cols(c), :])
            value = value.astype(BF16)
            mid_ref[:, cols(c)] = value
            value = value.astype(F32)
            return total + jnp.sum(value * value, axis=1, keepdims=True)

        total = lax.fori_loop(0, chunks, advance, jnp.zeros((tokens, 1), F32))
        inverse = lax.rsqrt(total / width + EPSILON)
        normalise(mid_ref, inverse)
        projections()
        q, k, v, probs, mixed = attention()
        rounded = probs.astype(BF16)
        dvalue = tn(rounded, dmixed).astype(BF16)
        dprobs = nt(dmixed, v)
        inner = jnp.sum(dprobs * probs, axis=1, keepdims=True)
        dscores = (probs * (dprobs - inner) * scale).astype(BF16)
        dq = nn(dscores, k).astype(BF16)
        dk = tn(dscores, q).astype(BF16)
        dall = jnp.concatenate([dq, dk, dvalue], axis=1)
        share = jnp.sum(dall.astype(F32) * acc_ref[...], axis=1, keepdims=True)
        share = share * inverse * inverse / width
        acc_ref[...] = jnp.zeros_like(acc_ref)

        def retreat(c, carry):
            dnorm = nt(dall, g_ref[cols(c), pl.ds(0, 3 * hd)])
            cot = jnp.where(valid, x_ref[:, cols(c)].astype(F32), 0.0)
            cot = cot + dnorm * inverse * gain_ref[:, cols(c)].astype(F32)
            cot = (cot - mid_ref[:, cols(c)].astype(F32) * share).astype(BF16)
            acc_ref[:, 0:hd] += nn(cot, wo_ref[cols(c), :])
            acc_ref[:, hd : hd + rank] += nt(cot, wide_ref[:, cols(c)])
            return carry

        lax.fori_loop(0, chunks, retreat, 0)
        back_ref[:, 0:hd] = acc_ref[:, 0:hd].astype(BF16)
        back_ref[:, hd : 2 * hd] = jnp.where(valid, acc_ref[:, hd : 2 * hd], 0.0).astype(BF16)
        give_back.start()
        finish(mixed, dvalue, wide_out)
        give_back.wait_send()

    def spread(i, carry):
        pltpu.make_async_remote_copy(
            src_ref=blk_ref, dst_ref=all_ref.at[me], send_sem=blk_send, recv_sem=blk_recv,
            device_id={"dp": (me + i) % n}, device_id_type=MESH,
        ).start()
        return carry

    lax.fori_loop(1, n, spread, 0)
    all_ref[me] = blk_ref[...]

    def everyone(ref, send, recv):
        return pltpu.make_async_remote_copy(
            src_ref=ref.at[pl.ds(0, n - 1)], dst_ref=ref.at[pl.ds(0, n - 1)],
            send_sem=send, recv_sem=recv, device_id={"dp": nxt}, device_id_type=MESH,
        )

    told = everyone(own_all, own_send, own_recv)
    told.wait_recv()
    pick_ref[...] = jnp.zeros_like(pick_ref)
    shared = everyone(all_ref, blk_send, blk_recv)
    shared.wait_recv()

    def choose(i, seen):
        for e in range(examples):
            named = jnp.where(own_all[i, pl.ds(e, 1), :] == me, 1.0, 0.0)
            piece = all_ref[i, e].astype(F32)
            for slot in range(CAP):
                weight = jnp.where(seen == float(slot), named, 0.0)
                pick_ref[slot] += weight * piece
            seen = seen + named
        return seen

    lax.fori_loop(0, n, choose, jnp.zeros((1, 2 * rank), F32))
    for slot in range(CAP):
        out_ref[slot, 0] = pick_ref[slot, :, 0:rank].astype(BF16)
        out_ref[slot, 1] = pick_ref[slot, :, rank : 2 * rank].astype(BF16)

    told.wait_send()
    shared.wait_send()

    def drain(s, carry):
        cw(s, place).wait_send()
        ccw(s, place).wait_send()
        over(s + 1, place, mine).wait_send()
        return carry

    lax.fori_loop(0, n - 1, drain, 0)


def shards(
    boundary, w_query, w_key, w_value, w_out, norm_gain, proj_wide, proj_head, lengths, owners
):
    n = lax.axis_size("dp")
    examples, length, width = boundary.shape[1:]
    rows, hd = w_query.shape[1:]
    rank = proj_wide.shape[0]
    tokens = examples * length
    chunk = min(width, 1024)
    weights = jnp.concatenate([w_query[0], w_key[0], w_value[0], w_out[0].T], axis=1)
    padded = -(-examples // 8) * 8
    own = jnp.pad(owners, ((0, padded - examples), (0, 0)))
    own = jnp.broadcast_to(own, (padded, 2 * rank))
    vmem = pl.BlockSpec(memory_space=pltpu.VMEM)
    dma = pltpu.SemaphoreType.DMA
    out = pl.pallas_call(
        functools.partial(kernel, n, examples, length, chunk),
        out_shape=jax.ShapeDtypeStruct((CAP, 2, rank, rank), BF16),
        in_specs=[
            pl.BlockSpec(memory_space=pltpu.SMEM), pl.BlockSpec(memory_space=pl.ANY),
            vmem, vmem, vmem, vmem, vmem,
        ],
        out_specs=vmem,
        scratch_shapes=[
            pltpu.VMEM((width, 4 * hd), BF16),
            pltpu.VMEM((width, hd), BF16),
            pltpu.VMEM((tokens, width), BF16),
            pltpu.VMEM((tokens, width), BF16),
            pltpu.VMEM((tokens, width), BF16),
            pltpu.VMEM((tokens, 3 * hd), F32),
            pltpu.VMEM((tokens, rank), F32),
            pltpu.VMEM((tokens, tokens), BF16),
            pltpu.VMEM((tokens, hd), BF16),
            pltpu.VMEM((tokens, 2 * hd), BF16),
            pltpu.VMEM((tokens, hd), BF16),
            pltpu.VMEM((tokens, 2 * hd), BF16),
            pltpu.VMEM((examples, rank, 2 * rank), BF16),
            pltpu.VMEM((n, examples, rank, 2 * rank), BF16),
            pltpu.VMEM((n, padded, 2 * rank), jnp.int32),
            pltpu.VMEM((CAP, rank, 2 * rank), F32),
            dma, dma, dma((n,)), dma((n,)), dma((n,)), dma, dma,
            dma, dma, dma, dma, dma, dma,
            dma, dma, dma, dma,
        ],
        compiler_params=pltpu.CompilerParams(
            collective_id=0, has_side_effects=True, vmem_limit_bytes=56 * 1024 * 1024
        ),
    )(
        lengths, weights, boundary.reshape(tokens, width), norm_gain,
        proj_wide, proj_head[0], own,
    )
    return out[:, None]


def solution(mesh):
    return jax.shard_map(
        shards,
        mesh=mesh,
        in_specs=(
            P("section", ("groups", "dp"), None, None),
            P("section", "dp", None),
            P("section", "dp", None),
            P("section", "dp", None),
            P("section", None, "dp"),
            P("section", None),
            P(),
            P("section", None, None, None),
            P(("groups", "dp")),
            P(("groups", "dp"), None),
        ),
        out_specs=P(("groups", "dp"), "section", None, None, None),
        check_vma=False,
    )
```

```python
import functools

import jax
import jax.numpy as jnp
from jax import lax
from jax.experimental import pallas as pl
from jax.experimental.pallas import tpu as pltpu
from jax.sharding import PartitionSpec as P

CAP = 4
EPSILON = 1e-05
MASKED = -1e30
MESH = pl.DeviceIdType.MESH
F32 = jnp.float32
BF16 = jnp.bfloat16


def nn(a, b):
    return lax.dot_general(a, b, (((1,), (0,)), ((), ())), preferred_element_type=F32)


def nt(a, b):
    return lax.dot_general(a, b, (((1,), (1,)), ((), ())), preferred_element_type=F32)


def tn(a, b):
    return lax.dot_general(a, b, (((0,), (0,)), ((), ())), preferred_element_type=F32)


def kernel(
    n, examples, length, parts,
    len_ref, w_ref, x_ref, gain_ref, wide_ref, head_ref, own_ref,
    out_ref,
    g_ref, wo_ref, left_ref, accl_ref, accm_ref, accc_ref, pre_ref, acc_ref, sq_ref,
    pin_ref, prb_ref, mix_ref, back_ref, mixin_ref, backin_ref, blk_ref, all_ref,
    own_all, pick_ref,
    loc_sem, send_sem, cw_sem, ccw_sem, y_sem, wo_send, wo_recv,
    x_send, x_recv, mix_send, mix_recv, back_send, back_recv,
    own_send, own_recv, blk_send, blk_recv,
):
    group = lax.axis_index("groups")
    me = lax.axis_index("dp")
    sec = lax.axis_index("section")
    rows = w_ref.shape[0]
    tokens, width = x_ref.shape
    hd = wo_ref.shape[1]
    rank = wide_ref.shape[0]
    third = rows // 3 // 16 * 16
    mid = rows - 2 * third
    mine = group * (rows - third)
    theirs = (1 - group) * (rows - third)
    half = n // 2
    parity = me % 2
    place = me // 2 + parity * (n - 1 - 2 * (me // 2))

    def pieces(size):
        if parts == 1:
            return ((0, size),)
        first = (size // 2 + 15) // 16 * 16
        return ((0, first), (first, size - first))

    side, middle = pieces(third), pieces(mid)

    def at(position):
        position = (position + 2 * n) % n
        high = position // half
        return (1 - high) * 2 * position + high * (2 * (n - 1 - position) + 1)

    nxt, prv = at(place + 1), at(place - 1)

    barrier = pltpu.get_barrier_semaphore()

    def greet(i, carry):
        pl.semaphore_signal(
            barrier, inc=1, device_id={"dp": (me + i) % n}, device_id_type=MESH
        )
        return carry

    own_block = pltpu.make_async_copy(w_ref, g_ref.at[pl.ds(me * rows, rows)], loc_sem)
    own_block.start()
    lax.fori_loop(1, n, greet, 0)
    pl.semaphore_signal(barrier, inc=1, device_id={"groups": 1 - group}, device_id_type=MESH)
    pl.semaphore_signal(barrier, inc=1, device_id={"section": 1 - sec}, device_id_type=MESH)
    own_block.wait()
    pl.semaphore_wait(barrier, n + 1)

    def part(origin, offset, size):
        return g_ref.at[pl.ds(pl.multiple_of(origin * rows + offset, 16), size)]

    def hop(ref, sem, target):
        return pltpu.make_async_remote_copy(
            src_ref=ref, dst_ref=ref, send_sem=send_sem, recv_sem=sem,
            device_id=target, device_id_type=MESH,
        )

    def cw(s, j, origin):
        offset, size = side[j]
        return hop(part(at(origin), mine + offset, size), cw_sem.at[s * parts + j], {"dp": nxt})

    def ccw(s, j, origin):
        offset, size = middle[j]
        return hop(
            part(at(origin), third + offset, size), ccw_sem.at[s * parts + j], {"dp": prv}
        )

    def over(s, j, origin, base):
        offset, size = side[j]
        return hop(
            part(at(origin), base + offset, size),
            y_sem.at[s * parts + j], {"groups": 1 - group},
        )

    def hand_over(index, offset, size):
        start = pl.multiple_of(at(place - index) * rows + offset, 16)

        @pl.when(sec == 0)
        def _():
            pltpu.make_async_remote_copy(
                src_ref=g_ref.at[pl.ds(start, size), pl.ds(3 * hd, hd)],
                dst_ref=wo_ref.at[pl.ds(start, size)],
                send_sem=wo_send, recv_sem=wo_recv.at[index],
                device_id={"section": 1 - sec}, device_id_type=MESH,
            ).start()

    def across(src, dst, send, recv):
        return pltpu.make_async_remote_copy(
            src_ref=src, dst_ref=dst, send_sem=send, recv_sem=recv,
            device_id={"section": 1 - sec}, device_id_type=MESH,
        )

    for j in range(parts):
        cw(0, j, place).start()
        ccw(0, j, place).start()
    give_x = across(x_ref, left_ref.at[pl.ds(0, tokens)], x_send, x_recv)

    @pl.when(sec == 0)
    def _():
        give_x.start()

    hand_over(0, 0, rows)

    def tell(i, carry):
        pltpu.make_async_remote_copy(
            src_ref=own_ref, dst_ref=own_all.at[me], send_sem=own_send, recv_sem=own_recv,
            device_id={"dp": (me + i) % n}, device_id_type=MESH,
        ).start()
        return carry

    lax.fori_loop(1, n, tell, 0)
    own_all[me] = own_ref[...]

    row = lax.broadcasted_iota(jnp.int32, (tokens, 1), 0)
    reach = jnp.zeros((tokens, 1), jnp.int32)
    for e in range(examples):
        reach = jnp.where(row // length == e, len_ref[e] + e * length, reach)
    valid = row < reach
    row2 = lax.broadcasted_iota(jnp.int32, (tokens, tokens), 0)
    col2 = lax.broadcasted_iota(jnp.int32, (tokens, tokens), 1)
    allowed = (col2 <= row2) & (col2 < reach) & (row2 // length == col2 // length)
    scale = hd ** (-0.5)
    chunk = min(width, 1024)
    chunks = width // chunk
    by_block = rows % 128 == 0
    t1, t2, t3, t4 = tokens, 2 * tokens, 2 * tokens + rank, 2 * tokens + 2 * rank

    def cols(c):
        return pl.ds(pl.multiple_of(c * chunk, chunk), chunk)

    accl_ref[...] = jnp.zeros_like(accl_ref)
    accm_ref[...] = jnp.zeros_like(accm_ref)
    accc_ref[...] = jnp.zeros_like(accc_ref)
    pre_ref[...] = jnp.zeros_like(pre_ref)
    acc_ref[...] = jnp.zeros_like(acc_ref)
    sq_ref[...] = jnp.zeros_like(sq_ref)

    def squares(value):
        value = value.astype(F32)
        sq_ref[...] += jnp.sum(value * value, axis=1, keepdims=True)

    @pl.when(sec == 0)
    def _():
        def one(c, carry):
            value = x_ref[:, cols(c)]
            squares(value)
            wide = wide_ref[:, cols(c)].astype(F32) * gain_ref[:, cols(c)].astype(F32)
            pre_ref[0:t1, 0:rank] += nt(value, wide.astype(BF16))
            return carry

        lax.fori_loop(0, chunks, one, 0)

    def prepare():
        give_x.wait_recv()

        def one(c, carry):
            value = left_ref[0:t1, cols(c)]
            squares(value)
            cot = jnp.where(valid, x_ref[:, cols(c)].astype(F32), 0.0).astype(BF16)
            left_ref[t1:t2, cols(c)] = cot
            plain = wide_ref[:, cols(c)]
            wide = plain.astype(F32) * gain_ref[:, cols(c)].astype(F32)
            left_ref[t2:t3, cols(c)] = plain
            left_ref[t3:t4, cols(c)] = wide.astype(BF16)
            pre_ref[0:t2] += nt(left_ref[0:t2, cols(c)], left_ref[t2:t4, cols(c)])
            return carry

        lax.fori_loop(0, chunks, one, 0)

    def contract(start, size):
        start = pl.multiple_of(start, size)
        span = pl.ds(start, size)

        @pl.when(sec == 0)
        def _():
            acc_ref[...] += nn(x_ref[:, span], g_ref[span, pl.ds(0, 3 * hd)])

        @pl.when(sec == 1)
        def _():
            wide_w = g_ref[span, pl.ds(0, 3 * hd)]
            out_w = wo_ref[span]
            turned = out_w.T
            left = left_ref[:, span]
            accl_ref[:, 0 : 3 * hd] += nn(left, wide_w)
            accl_ref[:, 3 * hd : 4 * hd] += nn(left, out_w)
            accm_ref[:, 0 : 3 * hd] += nn(turned, wide_w)
            accm_ref[:, 3 * hd : 4 * hd] += nn(turned, out_w)
            accc_ref[...] += nn(left_ref[t1:t2, span], g_ref[span, pl.ds(3 * hd, hd)])

    def handed(index):
        span = pl.ds(pl.multiple_of(at(place - index) * rows, rows), rows)

        @pl.when(sec == 1)
        def _():
            across(wo_ref.at[span], wo_ref.at[span], wo_send, wo_recv.at[index]).wait_recv()

    def block(index):
        if by_block:
            handed(index)
            contract(at(place - index) * rows, rows)

    def arrive(s, j):
        cw(s - 1, j, place - s).wait_recv()

        @pl.when(s < n - 1)
        def _():
            cw(s, j, place - s).start()

        over(s, j, place - s, mine).start()
        offset, size = side[j]
        hand_over(s, mine + offset, size)
        ccw(s - 1, j, place + s).wait_recv()

        @pl.when(s < n - 1)
        def _():
            ccw(s, j, place + s).start()

        offset, size = middle[j]
        hand_over(n - s, third + offset, size)

    def take(s, j):
        over(s, j, place - s, theirs).wait_recv()
        offset, size = side[j]
        hand_over(s, theirs + offset, size)

    def step(s, carry):
        for j in range(parts):
            arrive(s, j)

            @pl.when(s >= 2)
            def _():
                take(s - 1, j)

            if j == 0:
                @pl.when(s > half + 1)
                def _():
                    block(n - s + 1)

            if j == parts - 1:
                @pl.when(s > half)
                def _():
                    block(s - 1)

        @pl.when(s == 2)
        def _():
            @pl.when(sec == 1)
            def _():
                prepare()

            block(0)

        return carry

    lax.fori_loop(1, n, step, 0)
    block(1)
    for j in range(parts):
        take(n - 1, j)
    block(n - 1)
    if not by_block:
        def wait_for(s, carry):
            handed(s)
            return carry

        lax.fori_loop(0, n, wait_for, 0)

        def later(c, carry):
            contract(c * chunk, chunk)
            return carry

        lax.fori_loop(0, chunks, later, 0)

    def attention():
        q = acc_ref[:, 0:hd].astype(BF16)
        k = acc_ref[:, hd : 2 * hd].astype(BF16)
        v = acc_ref[:, 2 * hd : 3 * hd].astype(BF16)
        scores = jnp.where(allowed, nt(q, k) * scale, MASKED)
        raised = jnp.exp(scores - jnp.max(scores, axis=1, keepdims=True))
        probs = raised / jnp.sum(raised, axis=1, keepdims=True)
        mixed = nn(probs.astype(BF16), v).astype(BF16)
        return q, k, v, probs, mixed

    def finish(mixed, dvalue, wide_out):
        head_in = nt(mixed, head_ref[1]).astype(BF16)
        value_side = jnp.where(valid, nt(dvalue, head_ref[0]), 0.0).astype(BF16)
        wide_in = pin_ref[...].astype(BF16)
        for e in range(examples):
            span = slice(e * length, (e + 1) * length)
            first = tn(value_side[span], wide_in[span])
            second = tn(wide_out[span], head_in[span])
            blk_ref[e] = jnp.concatenate([first, second], axis=1).astype(BF16)

    give_mix = across(mix_ref, mixin_ref, mix_send, mix_recv)
    give_back = across(back_ref, backin_ref, back_send, back_recv)
    give_wo = across(wo_ref, wo_ref, wo_send, wo_recv.at[0])

    @pl.when(sec == 0)
    def _():
        inverse = lax.rsqrt(sq_ref[...] / width + EPSILON)
        acc_ref[...] = acc_ref[...] * inverse
        pin_ref[...] = pre_ref[0:t1, 0:rank] * inverse
        _, _, _, probs, mixed = attention()
        mix_ref[...] = mixed
        give_mix.start()
        prb_ref[...] = probs.astype(BF16)
        give_back.wait_recv()
        dmixed = backin_ref[:, 0:hd]
        wide_out = backin_ref[:, hd : hd + rank]
        dvalue = tn(prb_ref[...], dmixed).astype(BF16)
        finish(mix_ref[...], dvalue, wide_out)
        give_mix.wait_send()
        give_x.wait_send()
        give_wo.wait_send()

    @pl.when(sec == 1)
    def _():
        dmixed = accc_ref[...].astype(BF16)
        plain_out = pre_ref[t1:t2, 0:rank]
        give_mix.wait_recv()
        before = mixin_ref[...]
        moved = nn(before, accm_ref[...].astype(BF16))
        tilted = accl_ref[0:t1, 3 * hd : 4 * hd]
        square = moved[:, 3 * hd : 4 * hd] + 2.0 * tilted
        total = sq_ref[...] + jnp.sum(before.astype(F32) * square, axis=1, keepdims=True)
        inverse = lax.rsqrt(jnp.maximum(total, 0.0) / width + EPSILON)
        acc_ref[...] = (accl_ref[0:t1, 0 : 3 * hd] + moved[:, 0 : 3 * hd]) * inverse
        turned = nt(before, accl_ref[t2:t4, 3 * hd : 4 * hd].astype(BF16))
        pin_ref[...] = (pre_ref[0:t1, rank : 2 * rank] + turned[:, rank : 2 * rank]) * inverse
        q, k, v, probs, mixed = attention()
        rounded = probs.astype(BF16)
        dvalue = tn(rounded, dmixed).astype(BF16)
        dprobs = nt(dmixed, v)
        inner = jnp.sum(dprobs * probs, axis=1, keepdims=True)
        dscores = (probs * (dprobs - inner) * scale).astype(BF16)
        dq = nn(dscores, k).astype(BF16)
        dk = tn(dscores, q).astype(BF16)
        dall = jnp.concatenate([dq, dk, dvalue], axis=1)
        share = jnp.sum(dall.astype(F32) * acc_ref[...], axis=1, keepdims=True)
        share = share * inverse * inverse / width
        to_head = inverse * nt(dall, accm_ref[:, 0 : 3 * hd].astype(BF16))
        to_head = to_head - share * (tilted + moved[:, 3 * hd : 4 * hd])
        to_head = to_head + accl_ref[t1:t2, 3 * hd : 4 * hd]
        to_wide = inverse * nt(dall, accl_ref[t2:t3, 0 : 3 * hd].astype(BF16))
        to_wide = to_wide - share * (pre_ref[0:t1, 0:rank] + turned[:, 0:rank])
        to_wide = jnp.where(valid, to_wide + plain_out, 0.0)
        back_ref[:, 0:hd] = to_head.astype(BF16)
        back_ref[:, hd : hd + rank] = to_wide.astype(BF16)
        back_ref[:, hd + rank : 2 * hd] = jnp.zeros((tokens, hd - rank), BF16)
        give_back.start()
        finish(mixed, dvalue, plain_out.astype(BF16))
        give_back.wait_send()

    def spread(i, carry):
        pltpu.make_async_remote_copy(
            src_ref=blk_ref, dst_ref=all_ref.at[me], send_sem=blk_send, recv_sem=blk_recv,
            device_id={"dp": (me + i) % n}, device_id_type=MESH,
        ).start()
        return carry

    lax.fori_loop(1, n, spread, 0)
    all_ref[me] = blk_ref[...]

    def everyone(ref, send, recv):
        return pltpu.make_async_remote_copy(
            src_ref=ref.at[pl.ds(0, n - 1)], dst_ref=ref.at[pl.ds(0, n - 1)],
            send_sem=send, recv_sem=recv, device_id={"dp": nxt}, device_id_type=MESH,
        )

    told = everyone(own_all, own_send, own_recv)
    told.wait_recv()
    pick_ref[...] = jnp.zeros_like(pick_ref)
    shared = everyone(all_ref, blk_send, blk_recv)
    shared.wait_recv()

    def choose(i, seen):
        for e in range(examples):
            named = jnp.where(own_all[i, pl.ds(e, 1), :] == me, 1.0, 0.0)
            piece = all_ref[i, e].astype(F32)
            for slot in range(CAP):
                weight = jnp.where(seen == float(slot), named, 0.0)
                pick_ref[slot] += weight * piece
            seen = seen + named
        return seen

    lax.fori_loop(0, n, choose, jnp.zeros((1, 2 * rank), F32))
    for slot in range(CAP):
        out_ref[slot, 0] = pick_ref[slot, :, 0:rank].astype(BF16)
        out_ref[slot, 1] = pick_ref[slot, :, rank : 2 * rank].astype(BF16)

    told.wait_send()
    shared.wait_send()

    def drain(s, carry):
        for j in range(parts):
            cw(s, j, place).wait_send()
            ccw(s, j, place).wait_send()
            over(s + 1, j, place, mine).wait_send()
        return carry

    lax.fori_loop(0, n - 1, drain, 0)


def shards(
    boundary, w_query, w_key, w_value, w_out, norm_gain, proj_wide, proj_head, lengths, owners
):
    n = lax.axis_size("dp")
    examples, length, width = boundary.shape[1:]
    rows, hd = w_query.shape[1:]
    rank = proj_wide.shape[0]
    tokens = examples * length
    parts = 2 if rows >= 128 else 1
    gain = lax.dynamic_slice_in_dim(norm_gain[0], lax.axis_index("dp") * rows, rows)
    weights = jnp.concatenate([w_query[0], w_key[0], w_value[0]], axis=1)
    weights = (weights.astype(F32) * gain.astype(F32)[:, None]).astype(BF16)
    weights = jnp.concatenate([weights, w_out[0].T], axis=1)
    padded = -(-examples // 8) * 8
    own = jnp.pad(owners, ((0, padded - examples), (0, 0)))
    own = jnp.broadcast_to(own, (padded, 2 * rank))
    vmem = pl.BlockSpec(memory_space=pltpu.VMEM)
    dma = pltpu.SemaphoreType.DMA
    out = pl.pallas_call(
        functools.partial(kernel, n, examples, length, parts),
        out_shape=jax.ShapeDtypeStruct((CAP, 2, rank, rank), BF16),
        in_specs=[
            pl.BlockSpec(memory_space=pltpu.SMEM), pl.BlockSpec(memory_space=pl.ANY),
            vmem, vmem, vmem, vmem, vmem,
        ],
        out_specs=vmem,
        scratch_shapes=[
            pltpu.VMEM((width, 4 * hd), BF16),
            pltpu.VMEM((width, hd), BF16),
            pltpu.VMEM((2 * tokens + 2 * rank, width), BF16),
            pltpu.VMEM((2 * tokens + 2 * rank, 4 * hd), F32),
            pltpu.VMEM((hd, 4 * hd), F32),
            pltpu.VMEM((tokens, hd), F32),
            pltpu.VMEM((2 * tokens, 2 * rank), F32),
            pltpu.VMEM((tokens, 3 * hd), F32),
            pltpu.VMEM((tokens, 1), F32),
            pltpu.VMEM((tokens, rank), F32),
            pltpu.VMEM((tokens, tokens), BF16),
            pltpu.VMEM((tokens, hd), BF16),
            pltpu.VMEM((tokens, 2 * hd), BF16),
            pltpu.VMEM((tokens, hd), BF16),
            pltpu.VMEM((tokens, 2 * hd), BF16),
            pltpu.VMEM((examples, rank, 2 * rank), BF16),
            pltpu.VMEM((n, examples, rank, 2 * rank), BF16),
            pltpu.VMEM((n, padded, 2 * rank), jnp.int32),
            pltpu.VMEM((CAP, rank, 2 * rank), F32),
            dma, dma, dma((n * parts,)), dma((n * parts,)), dma((n * parts,)), dma, dma((n,)),
            dma, dma, dma, dma, dma, dma,
            dma, dma, dma, dma,
        ],
        compiler_params=pltpu.CompilerParams(
            collective_id=0, has_side_effects=True, vmem_limit_bytes=56 * 1024 * 1024
        ),
    )(
        lengths, weights, boundary.reshape(tokens, width), norm_gain,
        proj_wide, proj_head[0], own,
    )
    return out[:, None]


def solution(mesh):
    return jax.shard_map(
        shards,
        mesh=mesh,
        in_specs=(
            P("section", ("groups", "dp"), None, None),
            P("section", "dp", None),
            P("section", "dp", None),
            P("section", "dp", None),
            P("section", None, "dp"),
            P("section", None),
            P(),
            P("section", None, None, None),
            P(("groups", "dp")),
            P(("groups", "dp"), None),
        ),
        out_specs=P(("groups", "dp"), "section", None, None, None),
        check_vma=False,
    )
```

```python
import functools

import jax
import jax.numpy as jnp
from jax import lax
from jax.experimental import pallas as pl
from jax.experimental.pallas import tpu as pltpu
from jax.sharding import PartitionSpec as P

CAP = 4
EPSILON = 1e-05
MASKED = -1e30
MESH = pl.DeviceIdType.MESH
F32 = jnp.float32
BF16 = jnp.bfloat16


def nn(a, b):
    return lax.dot_general(a, b, (((1,), (0,)), ((), ())), preferred_element_type=F32)


def nt(a, b):
    return lax.dot_general(a, b, (((1,), (1,)), ((), ())), preferred_element_type=F32)


def tn(a, b):
    return lax.dot_general(a, b, (((0,), (0,)), ((), ())), preferred_element_type=F32)


def kernel(
    n, examples, length, parts,
    len_ref, owner_ref, wq_ref, wk_ref, wv_ref, wt_ref, near_ref, x_ref, gain_ref, wide_ref,
    head_ref,
    out_ref,
    g_ref, wo_ref, left_ref, accl_ref, accm_ref, accc_ref, pre_ref, acc_ref, sq_ref,
    pin_ref, prb_ref, mix_ref, back_ref, mixin_ref, backin_ref, blk_ref, all_ref,
    own_ref, own_all, pick_ref,
    send_sem, cw_sem, ccw_sem, y_sem, wo_send, wo_recv,
    x_send, x_recv, mix_send, mix_recv, back_send, back_recv,
    own_send, own_recv, blk_send, blk_recv,
):
    group = lax.axis_index("groups")
    me = lax.axis_index("dp")
    sec = lax.axis_index("section")
    rows = wq_ref.shape[0]
    tokens, width = x_ref.shape
    hd = wo_ref.shape[1]
    rank = wide_ref.shape[0]
    third = rows // 3 // 16 * 16
    mid = rows - 2 * third
    mine = group * (rows - third)
    theirs = (1 - group) * (rows - third)
    half = n // 2
    parity = me % 2
    place = me // 2 + parity * (n - 1 - 2 * (me // 2))

    def pieces(size):
        if parts == 1:
            return ((0, size),)
        first = (size // 2 + 15) // 16 * 16
        return ((0, first), (first, size - first))

    side, middle = pieces(third), pieces(mid)

    def at(position):
        position = (position + 2 * n) % n
        high = position // half
        return (1 - high) * 2 * position + high * (2 * (n - 1 - position) + 1)

    nxt, prv = at(place + 1), at(place - 1)

    barrier = pltpu.get_barrier_semaphore()

    def greet(i, carry):
        pl.semaphore_signal(
            barrier, inc=1, device_id={"dp": (me + i) % n}, device_id_type=MESH
        )
        return carry

    lax.fori_loop(1, n, greet, 0)
    pl.semaphore_signal(barrier, inc=1, device_id={"groups": 1 - group}, device_id_type=MESH)
    pl.semaphore_signal(barrier, inc=1, device_id={"section": 1 - sec}, device_id_type=MESH)
    base = pl.ds(pl.multiple_of(me * rows, rows), rows)
    by_block = rows % 128 == 0
    near = near_ref[:, base] if by_block else near_ref[...]
    near = jnp.broadcast_to(near.astype(F32), (hd, rows)).T
    for m, ref in enumerate((wq_ref, wk_ref, wv_ref)):
        g_ref[base, m * hd : (m + 1) * hd] = (ref[...].astype(F32) * near).astype(BF16)
    g_ref[base, 3 * hd : 4 * hd] = wt_ref[...].T
    own_ref[...] = jnp.zeros_like(own_ref)
    for e in range(examples):
        own_ref[e : e + 1] = jnp.full((1, 2 * rank), owner_ref[e, 0], jnp.int32)
    pl.semaphore_wait(barrier, n + 1)

    def part(origin, offset, size):
        return g_ref.at[pl.ds(pl.multiple_of(origin * rows + offset, 16), size)]

    def hop(ref, sem, target):
        return pltpu.make_async_remote_copy(
            src_ref=ref, dst_ref=ref, send_sem=send_sem, recv_sem=sem,
            device_id=target, device_id_type=MESH,
        )

    def cw(s, j, origin):
        offset, size = side[j]
        return hop(part(at(origin), mine + offset, size), cw_sem.at[s * parts + j], {"dp": nxt})

    def ccw(s, j, origin):
        offset, size = middle[j]
        return hop(
            part(at(origin), third + offset, size), ccw_sem.at[s * parts + j], {"dp": prv}
        )

    def over(s, j, origin, base):
        offset, size = side[j]
        return hop(
            part(at(origin), base + offset, size),
            y_sem.at[s * parts + j], {"groups": 1 - group},
        )

    def hand_over(index, offset, size):
        start = pl.multiple_of(at(place - index) * rows + offset, 16)

        @pl.when(sec == 0)
        def _():
            pltpu.make_async_remote_copy(
                src_ref=g_ref.at[pl.ds(start, size), pl.ds(3 * hd, hd)],
                dst_ref=wo_ref.at[pl.ds(start, size)],
                send_sem=wo_send, recv_sem=wo_recv.at[index],
                device_id={"section": 1 - sec}, device_id_type=MESH,
            ).start()

    def across(src, dst, send, recv):
        return pltpu.make_async_remote_copy(
            src_ref=src, dst_ref=dst, send_sem=send, recv_sem=recv,
            device_id={"section": 1 - sec}, device_id_type=MESH,
        )

    for j in range(parts):
        cw(0, j, place).start()
        ccw(0, j, place).start()
    give_x = across(x_ref, left_ref.at[pl.ds(0, tokens)], x_send, x_recv)

    @pl.when(sec == 0)
    def _():
        give_x.start()

    hand_over(0, 0, rows)

    def tell(i, carry):
        pltpu.make_async_remote_copy(
            src_ref=own_ref, dst_ref=own_all.at[me], send_sem=own_send, recv_sem=own_recv,
            device_id={"dp": (me + i) % n}, device_id_type=MESH,
        ).start()
        return carry

    lax.fori_loop(1, n, tell, 0)
    own_all[me] = own_ref[...]

    row = lax.broadcasted_iota(jnp.int32, (tokens, 1), 0)
    reach = jnp.zeros((tokens, 1), jnp.int32)
    for e in range(examples):
        reach = jnp.where(row // length == e, len_ref[e] + e * length, reach)
    valid = row < reach
    row2 = lax.broadcasted_iota(jnp.int32, (tokens, tokens), 0)
    col2 = lax.broadcasted_iota(jnp.int32, (tokens, tokens), 1)
    allowed = (col2 <= row2) & (col2 < reach) & (row2 // length == col2 // length)
    scale = hd ** (-0.5)
    chunk = min(width, 1024)
    chunks = width // chunk
    t1, t2, t3, t4 = tokens, 2 * tokens, 2 * tokens + rank, 2 * tokens + 2 * rank

    def cols(c):
        return pl.ds(pl.multiple_of(c * chunk, chunk), chunk)

    accl_ref[...] = jnp.zeros_like(accl_ref)
    accm_ref[...] = jnp.zeros_like(accm_ref)
    accc_ref[...] = jnp.zeros_like(accc_ref)
    pre_ref[...] = jnp.zeros_like(pre_ref)
    acc_ref[...] = jnp.zeros_like(acc_ref)
    sq_ref[...] = jnp.zeros_like(sq_ref)

    def squares(value):
        value = value.astype(F32)
        sq_ref[...] += jnp.sum(value * value, axis=1, keepdims=True)

    @pl.when(sec == 0)
    def _():
        def one(c, carry):
            value = x_ref[:, cols(c)]
            squares(value)
            wide = wide_ref[:, cols(c)].astype(F32) * gain_ref[:, cols(c)].astype(F32)
            pre_ref[0:t1, 0:rank] += nt(value, wide.astype(BF16))
            return carry

        lax.fori_loop(0, chunks, one, 0)

    def prepare():
        give_x.wait_recv()

        def one(c, carry):
            value = left_ref[0:t1, cols(c)]
            squares(value)
            cot = jnp.where(valid, x_ref[:, cols(c)].astype(F32), 0.0).astype(BF16)
            left_ref[t1:t2, cols(c)] = cot
            plain = wide_ref[:, cols(c)]
            wide = plain.astype(F32) * gain_ref[:, cols(c)].astype(F32)
            left_ref[t2:t3, cols(c)] = plain
            left_ref[t3:t4, cols(c)] = wide.astype(BF16)
            pre_ref[0:t2] += nt(left_ref[0:t2, cols(c)], left_ref[t2:t4, cols(c)])
            return carry

        lax.fori_loop(0, chunks, one, 0)

    def contract(start, size):
        start = pl.multiple_of(start, size)
        span = pl.ds(start, size)

        @pl.when(sec == 0)
        def _():
            acc_ref[...] += nn(x_ref[:, span], g_ref[span, pl.ds(0, 3 * hd)])

        @pl.when(sec == 1)
        def _():
            wide_w = g_ref[span, pl.ds(0, 3 * hd)]
            out_w = wo_ref[span]
            turned = out_w.T
            left = left_ref[:, span]
            accl_ref[:, 0 : 3 * hd] += nn(left, wide_w)
            accl_ref[:, 3 * hd : 4 * hd] += nn(left, out_w)
            accm_ref[:, 0 : 3 * hd] += nn(turned, wide_w)
            accm_ref[:, 3 * hd : 4 * hd] += nn(turned, out_w)
            accc_ref[...] += nn(left_ref[t1:t2, span], g_ref[span, pl.ds(3 * hd, hd)])

    def handed(index):
        span = pl.ds(pl.multiple_of(at(place - index) * rows, rows), rows)

        @pl.when(sec == 1)
        def _():
            across(wo_ref.at[span], wo_ref.at[span], wo_send, wo_recv.at[index]).wait_recv()

    def block(index):
        if by_block:
            handed(index)
            contract(at(place - index) * rows, rows)

    def arrive(s, j):
        cw(s - 1, j, place - s).wait_recv()

        @pl.when(s < n - 1)
        def _():
            cw(s, j, place - s).start()

        over(s, j, place - s, mine).start()
        offset, size = side[j]
        hand_over(s, mine + offset, size)
        ccw(s - 1, j, place + s).wait_recv()

        @pl.when(s < n - 1)
        def _():
            ccw(s, j, place + s).start()

        offset, size = middle[j]
        hand_over(n - s, third + offset, size)

    def take(s, j):
        over(s, j, place - s, theirs).wait_recv()
        offset, size = side[j]
        hand_over(s, theirs + offset, size)

    def step(s, carry):
        for j in range(parts):
            arrive(s, j)

            @pl.when(s >= 2)
            def _():
                take(s - 1, j)

            if j == 0:
                @pl.when(s > half + 1)
                def _():
                    block(n - s + 1)

            if j == parts - 1:
                @pl.when(s > half)
                def _():
                    block(s - 1)

        @pl.when(s == 2)
        def _():
            @pl.when(sec == 1)
            def _():
                prepare()

            block(0)

        return carry

    lax.fori_loop(1, n, step, 0)
    block(1)
    for j in range(parts):
        take(n - 1, j)
    block(n - 1)
    if not by_block:
        def wait_for(s, carry):
            handed(s)
            return carry

        lax.fori_loop(0, n, wait_for, 0)

        def later(c, carry):
            contract(c * chunk, chunk)
            return carry

        lax.fori_loop(0, chunks, later, 0)

    def attention():
        q = acc_ref[:, 0:hd].astype(BF16)
        k = acc_ref[:, hd : 2 * hd].astype(BF16)
        v = acc_ref[:, 2 * hd : 3 * hd].astype(BF16)
        scores = jnp.where(allowed, nt(q, k) * scale, MASKED)
        raised = jnp.exp(scores - jnp.max(scores, axis=1, keepdims=True))
        probs = raised / jnp.sum(raised, axis=1, keepdims=True)
        mixed = nn(probs.astype(BF16), v).astype(BF16)
        return q, k, v, probs, mixed

    def finish(mixed, dvalue, wide_out):
        head_in = nt(mixed, head_ref[1]).astype(BF16)
        value_side = jnp.where(valid, nt(dvalue, head_ref[0]), 0.0).astype(BF16)
        wide_in = pin_ref[...].astype(BF16)
        for e in range(examples):
            span = slice(e * length, (e + 1) * length)
            first = tn(value_side[span], wide_in[span])
            second = tn(wide_out[span], head_in[span])
            blk_ref[e] = jnp.concatenate([first, second], axis=1).astype(BF16)

    give_mix = across(mix_ref, mixin_ref, mix_send, mix_recv)
    give_back = across(back_ref, backin_ref, back_send, back_recv)
    give_wo = across(wo_ref, wo_ref, wo_send, wo_recv.at[0])

    @pl.when(sec == 0)
    def _():
        inverse = lax.rsqrt(sq_ref[...] / width + EPSILON)
        acc_ref[...] = acc_ref[...] * inverse
        pin_ref[...] = pre_ref[0:t1, 0:rank] * inverse
        _, _, _, probs, mixed = attention()
        mix_ref[...] = mixed
        give_mix.start()
        prb_ref[...] = probs.astype(BF16)
        give_back.wait_recv()
        dmixed = backin_ref[:, 0:hd]
        wide_out = backin_ref[:, hd : hd + rank]
        dvalue = tn(prb_ref[...], dmixed).astype(BF16)
        finish(mix_ref[...], dvalue, wide_out)
        give_mix.wait_send()
        give_x.wait_send()
        give_wo.wait_send()

    @pl.when(sec == 1)
    def _():
        dmixed = accc_ref[...].astype(BF16)
        plain_out = pre_ref[t1:t2, 0:rank]
        give_mix.wait_recv()
        before = mixin_ref[...]
        moved = nn(before, accm_ref[...].astype(BF16))
        tilted = accl_ref[0:t1, 3 * hd : 4 * hd]
        square = moved[:, 3 * hd : 4 * hd] + 2.0 * tilted
        total = sq_ref[...] + jnp.sum(before.astype(F32) * square, axis=1, keepdims=True)
        inverse = lax.rsqrt(jnp.maximum(total, 0.0) / width + EPSILON)
        acc_ref[...] = (accl_ref[0:t1, 0 : 3 * hd] + moved[:, 0 : 3 * hd]) * inverse
        turned = nt(before, accl_ref[t2:t4, 3 * hd : 4 * hd].astype(BF16))
        pin_ref[...] = (pre_ref[0:t1, rank : 2 * rank] + turned[:, rank : 2 * rank]) * inverse
        q, k, v, probs, mixed = attention()
        rounded = probs.astype(BF16)
        dvalue = tn(rounded, dmixed).astype(BF16)
        dprobs = nt(dmixed, v)
        inner = jnp.sum(dprobs * probs, axis=1, keepdims=True)
        dscores = (probs * (dprobs - inner) * scale).astype(BF16)
        dq = nn(dscores, k).astype(BF16)
        dk = tn(dscores, q).astype(BF16)
        dall = jnp.concatenate([dq, dk, dvalue], axis=1)
        share = jnp.sum(dall.astype(F32) * acc_ref[...], axis=1, keepdims=True)
        share = share * inverse * inverse / width
        to_head = inverse * nt(dall, accm_ref[:, 0 : 3 * hd].astype(BF16))
        to_head = to_head - share * (tilted + moved[:, 3 * hd : 4 * hd])
        to_head = to_head + accl_ref[t1:t2, 3 * hd : 4 * hd]
        to_wide = inverse * nt(dall, accl_ref[t2:t3, 0 : 3 * hd].astype(BF16))
        to_wide = to_wide - share * (pre_ref[0:t1, 0:rank] + turned[:, 0:rank])
        to_wide = jnp.where(valid, to_wide + plain_out, 0.0)
        back_ref[:, 0:hd] = to_head.astype(BF16)
        back_ref[:, hd : hd + rank] = to_wide.astype(BF16)
        back_ref[:, hd + rank : 2 * hd] = jnp.zeros((tokens, hd - rank), BF16)
        give_back.start()
        finish(mixed, dvalue, plain_out.astype(BF16))
        give_back.wait_send()

    def spread(i, carry):
        pltpu.make_async_remote_copy(
            src_ref=blk_ref, dst_ref=all_ref.at[me], send_sem=blk_send, recv_sem=blk_recv,
            device_id={"dp": (me + i) % n}, device_id_type=MESH,
        ).start()
        return carry

    lax.fori_loop(1, n, spread, 0)
    all_ref[me] = blk_ref[...]

    def everyone(ref, send, recv):
        return pltpu.make_async_remote_copy(
            src_ref=ref.at[pl.ds(0, n - 1)], dst_ref=ref.at[pl.ds(0, n - 1)],
            send_sem=send, recv_sem=recv, device_id={"dp": nxt}, device_id_type=MESH,
        )

    told = everyone(own_all, own_send, own_recv)
    told.wait_recv()
    pick_ref[...] = jnp.zeros_like(pick_ref)
    shared = everyone(all_ref, blk_send, blk_recv)
    shared.wait_recv()

    def choose(i, seen):
        for e in range(examples):
            named = jnp.where(own_all[i, pl.ds(e, 1), :] == me, 1.0, 0.0)
            piece = all_ref[i, e].astype(F32)
            for slot in range(CAP):
                weight = jnp.where(seen == float(slot), named, 0.0)
                pick_ref[slot] += weight * piece
            seen = seen + named
        return seen

    lax.fori_loop(0, n, choose, jnp.zeros((1, 2 * rank), F32))
    for slot in range(CAP):
        out_ref[slot, 0] = pick_ref[slot, :, 0:rank].astype(BF16)
        out_ref[slot, 1] = pick_ref[slot, :, rank : 2 * rank].astype(BF16)

    told.wait_send()
    shared.wait_send()

    def drain(s, carry):
        for j in range(parts):
            cw(s, j, place).wait_send()
            ccw(s, j, place).wait_send()
            over(s + 1, j, place, mine).wait_send()
        return carry

    lax.fori_loop(0, n - 1, drain, 0)


def shards(
    boundary, w_query, w_key, w_value, w_out, norm_gain, proj_wide, proj_head, lengths, owners
):
    n = lax.axis_size("dp")
    examples, length, width = boundary.shape[1:]
    rows, hd = w_query.shape[1:]
    rank = proj_wide.shape[0]
    tokens = examples * length
    parts = 2 if rows >= 128 else 1
    near = norm_gain
    if rows % 128:
        near = lax.dynamic_slice_in_dim(near, lax.axis_index("dp") * rows, rows, axis=1)
    padded = -(-examples // 8) * 8
    vmem = pl.BlockSpec(memory_space=pltpu.VMEM)
    smem = pl.BlockSpec(memory_space=pltpu.SMEM)
    dma = pltpu.SemaphoreType.DMA
    out = pl.pallas_call(
        functools.partial(kernel, n, examples, length, parts),
        out_shape=jax.ShapeDtypeStruct((CAP, 2, rank, rank), BF16),
        in_specs=[
            smem, smem, vmem, vmem, vmem, vmem, vmem, vmem, vmem, vmem, vmem,
        ],
        out_specs=vmem,
        scratch_shapes=[
            pltpu.VMEM((width, 4 * hd), BF16),
            pltpu.VMEM((width, hd), BF16),
            pltpu.VMEM((2 * tokens + 2 * rank, width), BF16),
            pltpu.VMEM((2 * tokens + 2 * rank, 4 * hd), F32),
            pltpu.VMEM((hd, 4 * hd), F32),
            pltpu.VMEM((tokens, hd), F32),
            pltpu.VMEM((2 * tokens, 2 * rank), F32),
            pltpu.VMEM((tokens, 3 * hd), F32),
            pltpu.VMEM((tokens, 1), F32),
            pltpu.VMEM((tokens, rank), F32),
            pltpu.VMEM((tokens, tokens), BF16),
            pltpu.VMEM((tokens, hd), BF16),
            pltpu.VMEM((tokens, 2 * hd), BF16),
            pltpu.VMEM((tokens, hd), BF16),
            pltpu.VMEM((tokens, 2 * hd), BF16),
            pltpu.VMEM((examples, rank, 2 * rank), BF16),
            pltpu.VMEM((n, examples, rank, 2 * rank), BF16),
            pltpu.VMEM((padded, 2 * rank), jnp.int32),
            pltpu.VMEM((n, padded, 2 * rank), jnp.int32),
            pltpu.VMEM((CAP, rank, 2 * rank), F32),
            dma, dma((n * parts,)), dma((n * parts,)), dma((n * parts,)), dma, dma((n,)),
            dma, dma, dma, dma, dma, dma,
            dma, dma, dma, dma,
        ],
        compiler_params=pltpu.CompilerParams(
            collective_id=0, has_side_effects=True, vmem_limit_bytes=56 * 1024 * 1024
        ),
    )(
        lengths, owners, w_query[0], w_key[0], w_value[0], w_out[0], near,
        boundary.reshape(tokens, width), norm_gain, proj_wide, proj_head[0],
    )
    return out[:, None]


def solution(mesh):
    return jax.shard_map(
        shards,
        mesh=mesh,
        in_specs=(
            P("section", ("groups", "dp"), None, None),
            P("section", "dp", None),
            P("section", "dp", None),
            P("section", "dp", None),
            P("section", None, "dp"),
            P("section", None),
            P(),
            P("section", None, None, None),
            P(("groups", "dp")),
            P(("groups", "dp"), None),
        ),
        out_specs=P(("groups", "dp"), "section", None, None, None),
        check_vma=False,
    )
```

```python
import functools

import jax
import jax.numpy as jnp
from jax import lax
from jax.experimental import pallas as pl
from jax.experimental.pallas import tpu as pltpu
from jax.sharding import PartitionSpec as P

CAP = 4
EPSILON = 1e-05
MASKED = -1e30
MESH = pl.DeviceIdType.MESH
F32 = jnp.float32
BF16 = jnp.bfloat16


def nn(a, b):
    return lax.dot_general(a, b, (((1,), (0,)), ((), ())), preferred_element_type=F32)


def nt(a, b):
    return lax.dot_general(a, b, (((1,), (1,)), ((), ())), preferred_element_type=F32)


def tn(a, b):
    return lax.dot_general(a, b, (((0,), (0,)), ((), ())), preferred_element_type=F32)


def kernel(
    n, examples, length, parts,
    len_ref, owner_ref, wq_ref, wk_ref, wv_ref, wt_ref, near_ref, x_ref, gain_ref, wide_ref,
    head_ref,
    out_ref,
    g_ref, wo_ref, left_ref, accl_ref, accm_ref, accc_ref, pre_ref, acc_ref, sq_ref,
    pin_ref, prb_ref, mix_ref, back_ref, mixin_ref, backin_ref, blk_ref, all_ref,
    own_ref, own_all, pick_ref,
    send_sem, cw_sem, ccw_sem, y_sem, wo_send, wo_recv,
    x_send, x_recv, mix_send, mix_recv, back_send, back_recv,
    own_send, own_recv, blk_send, blk_recv,
):
    group = lax.axis_index("groups")
    me = lax.axis_index("dp")
    sec = lax.axis_index("section")
    rows = wq_ref.shape[0]
    tokens, width = x_ref.shape
    hd = wo_ref.shape[1]
    rank = wide_ref.shape[0]
    third = rows // 3 // 16 * 16
    mid = rows - 2 * third
    mine = group * (rows - third)
    theirs = (1 - group) * (rows - third)
    half = n // 2
    parity = me % 2
    place = me // 2 + parity * (n - 1 - 2 * (me // 2))

    def pieces(size):
        if parts == 1:
            return ((0, size),)
        first = (size // 2 + 15) // 16 * 16
        return ((0, first), (first, size - first))

    side, middle = pieces(third), pieces(mid)

    def at(position):
        position = (position + 2 * n) % n
        high = position // half
        return (1 - high) * 2 * position + high * (2 * (n - 1 - position) + 1)

    nxt, prv = at(place + 1), at(place - 1)

    barrier = pltpu.get_barrier_semaphore()

    def greet(i, carry):
        pl.semaphore_signal(
            barrier, inc=1, device_id={"dp": (me + i) % n}, device_id_type=MESH
        )
        return carry

    lax.fori_loop(1, n, greet, 0)
    pl.semaphore_signal(barrier, inc=1, device_id={"groups": 1 - group}, device_id_type=MESH)
    pl.semaphore_signal(barrier, inc=1, device_id={"section": 1 - sec}, device_id_type=MESH)
    base = pl.ds(pl.multiple_of(me * rows, rows), rows)
    by_block = rows % 128 == 0
    near = near_ref[:, base] if by_block else near_ref[...]
    near = jnp.broadcast_to(near.astype(F32), (hd, rows)).T
    for m, ref in enumerate((wq_ref, wk_ref, wv_ref)):
        g_ref[base, m * hd : (m + 1) * hd] = (ref[...].astype(F32) * near).astype(BF16)
    g_ref[base, 3 * hd : 4 * hd] = wt_ref[...].T
    own_ref[...] = jnp.zeros_like(own_ref)
    for e in range(examples):
        own_ref[e : e + 1] = jnp.full((1, 2 * rank), owner_ref[0, e], jnp.int32)
    pl.semaphore_wait(barrier, n + 1)

    def part(origin, offset, size):
        return g_ref.at[pl.ds(pl.multiple_of(origin * rows + offset, 16), size)]

    def hop(ref, sem, target):
        return pltpu.make_async_remote_copy(
            src_ref=ref, dst_ref=ref, send_sem=send_sem, recv_sem=sem,
            device_id=target, device_id_type=MESH,
        )

    def cw(s, j, origin):
        offset, size = side[j]
        return hop(part(at(origin), mine + offset, size), cw_sem.at[s * parts + j], {"dp": nxt})

    def ccw(s, j, origin):
        offset, size = middle[j]
        return hop(
            part(at(origin), third + offset, size), ccw_sem.at[s * parts + j], {"dp": prv}
        )

    def over(s, j, origin, base):
        offset, size = side[j]
        return hop(
            part(at(origin), base + offset, size),
            y_sem.at[s * parts + j], {"groups": 1 - group},
        )

    def hand_over(index, offset, size):
        start = pl.multiple_of(at(place - index) * rows + offset, 16)

        @pl.when(sec == 0)
        def _():
            pltpu.make_async_remote_copy(
                src_ref=g_ref.at[pl.ds(start, size), pl.ds(3 * hd, hd)],
                dst_ref=wo_ref.at[pl.ds(start, size)],
                send_sem=wo_send, recv_sem=wo_recv.at[index],
                device_id={"section": 1 - sec}, device_id_type=MESH,
            ).start()

    def across(src, dst, send, recv):
        return pltpu.make_async_remote_copy(
            src_ref=src, dst_ref=dst, send_sem=send, recv_sem=recv,
            device_id={"section": 1 - sec}, device_id_type=MESH,
        )

    for j in range(parts):
        cw(0, j, place).start()
        ccw(0, j, place).start()
    give_x = across(x_ref, left_ref.at[pl.ds(0, tokens)], x_send, x_recv)

    @pl.when(sec == 0)
    def _():
        give_x.start()

    hand_over(0, 0, rows)

    def tell(i, carry):
        pltpu.make_async_remote_copy(
            src_ref=own_ref, dst_ref=own_all.at[me], send_sem=own_send, recv_sem=own_recv,
            device_id={"dp": (me + i) % n}, device_id_type=MESH,
        ).start()
        return carry

    lax.fori_loop(1, n, tell, 0)
    own_all[me] = own_ref[...]

    row = lax.broadcasted_iota(jnp.int32, (tokens, 1), 0)
    reach = jnp.zeros((tokens, 1), jnp.int32)
    for e in range(examples):
        reach = jnp.where(row // length == e, len_ref[e] + e * length, reach)
    valid = row < reach
    row2 = lax.broadcasted_iota(jnp.int32, (tokens, tokens), 0)
    col2 = lax.broadcasted_iota(jnp.int32, (tokens, tokens), 1)
    allowed = (col2 <= row2) & (col2 < reach) & (row2 // length == col2 // length)
    scale = hd ** (-0.5)
    chunk = min(width, 1024)
    chunks = width // chunk
    t1, t2, t3, t4 = tokens, 2 * tokens, 2 * tokens + rank, 2 * tokens + 2 * rank

    def cols(c):
        return pl.ds(pl.multiple_of(c * chunk, chunk), chunk)

    accl_ref[...] = jnp.zeros_like(accl_ref)
    accm_ref[...] = jnp.zeros_like(accm_ref)
    accc_ref[...] = jnp.zeros_like(accc_ref)
    pre_ref[...] = jnp.zeros_like(pre_ref)
    acc_ref[...] = jnp.zeros_like(acc_ref)
    sq_ref[...] = jnp.zeros_like(sq_ref)

    def squares(value):
        value = value.astype(F32)
        sq_ref[...] += jnp.sum(value * value, axis=1, keepdims=True)

    @pl.when(sec == 0)
    def _():
        def one(c, carry):
            value = x_ref[:, cols(c)]
            squares(value)
            wide = wide_ref[:, cols(c)].astype(F32) * gain_ref[:, cols(c)].astype(F32)
            pre_ref[0:t1, 0:rank] += nt(value, wide.astype(BF16))
            return carry

        lax.fori_loop(0, chunks, one, 0)

    def prepare():
        give_x.wait_recv()

        def one(c, carry):
            value = left_ref[0:t1, cols(c)]
            squares(value)
            cot = jnp.where(valid, x_ref[:, cols(c)].astype(F32), 0.0).astype(BF16)
            left_ref[t1:t2, cols(c)] = cot
            plain = wide_ref[:, cols(c)]
            wide = plain.astype(F32) * gain_ref[:, cols(c)].astype(F32)
            left_ref[t2:t3, cols(c)] = plain
            left_ref[t3:t4, cols(c)] = wide.astype(BF16)
            pre_ref[0:t2] += nt(left_ref[0:t2, cols(c)], left_ref[t2:t4, cols(c)])
            return carry

        lax.fori_loop(0, chunks, one, 0)

    def contract(start, size):
        start = pl.multiple_of(start, size)
        span = pl.ds(start, size)

        @pl.when(sec == 0)
        def _():
            acc_ref[...] += nn(x_ref[:, span], g_ref[span, pl.ds(0, 3 * hd)])

        @pl.when(sec == 1)
        def _():
            wide_w = g_ref[span, pl.ds(0, 3 * hd)]
            out_w = wo_ref[span]
            turned = out_w.T
            left = left_ref[:, span]
            accl_ref[:, 0 : 3 * hd] += nn(left, wide_w)
            accl_ref[:, 3 * hd : 4 * hd] += nn(left, out_w)
            accm_ref[:, 0 : 3 * hd] += nn(turned, wide_w)
            accm_ref[:, 3 * hd : 4 * hd] += nn(turned, out_w)
            accc_ref[...] += nn(left_ref[t1:t2, span], g_ref[span, pl.ds(3 * hd, hd)])

    def handed(index):
        span = pl.ds(pl.multiple_of(at(place - index) * rows, rows), rows)

        @pl.when(sec == 1)
        def _():
            across(wo_ref.at[span], wo_ref.at[span], wo_send, wo_recv.at[index]).wait_recv()

    def block(index):
        if by_block:
            handed(index)
            contract(at(place - index) * rows, rows)

    def arrive(s, j):
        cw(s - 1, j, place - s).wait_recv()

        @pl.when(s < n - 1)
        def _():
            cw(s, j, place - s).start()

        over(s, j, place - s, mine).start()
        offset, size = side[j]
        hand_over(s, mine + offset, size)
        ccw(s - 1, j, place + s).wait_recv()

        @pl.when(s < n - 1)
        def _():
            ccw(s, j, place + s).start()

        offset, size = middle[j]
        hand_over(n - s, third + offset, size)

    def take(s, j):
        over(s, j, place - s, theirs).wait_recv()
        offset, size = side[j]
        hand_over(s, theirs + offset, size)

    def step(s, carry):
        for j in range(parts):
            arrive(s, j)

            @pl.when(s >= 2)
            def _():
                take(s - 1, j)

            if j == 0:
                @pl.when(s > half + 1)
                def _():
                    block(n - s + 1)

            if j == parts - 1:
                @pl.when(s > half)
                def _():
                    block(s - 1)

        @pl.when(s == 2)
        def _():
            @pl.when(sec == 1)
            def _():
                prepare()

            block(0)

        return carry

    lax.fori_loop(1, n, step, 0)
    block(1)
    for j in range(parts):
        take(n - 1, j)
    block(n - 1)
    if not by_block:
        def wait_for(s, carry):
            handed(s)
            return carry

        lax.fori_loop(0, n, wait_for, 0)

        def later(c, carry):
            contract(c * chunk, chunk)
            return carry

        lax.fori_loop(0, chunks, later, 0)

    def attention():
        q = acc_ref[:, 0:hd].astype(BF16)
        k = acc_ref[:, hd : 2 * hd].astype(BF16)
        v = acc_ref[:, 2 * hd : 3 * hd].astype(BF16)
        scores = jnp.where(allowed, nt(q, k) * scale, MASKED)
        raised = jnp.exp(scores - jnp.max(scores, axis=1, keepdims=True))
        probs = raised / jnp.sum(raised, axis=1, keepdims=True)
        mixed = nn(probs.astype(BF16), v).astype(BF16)
        return q, k, v, probs, mixed

    def finish(mixed, dvalue, wide_out):
        head_in = nt(mixed, head_ref[1]).astype(BF16)
        value_side = jnp.where(valid, nt(dvalue, head_ref[0]), 0.0).astype(BF16)
        wide_in = pin_ref[...].astype(BF16)
        for e in range(examples):
            span = slice(e * length, (e + 1) * length)
            first = tn(value_side[span], wide_in[span])
            second = tn(wide_out[span], head_in[span])
            blk_ref[e] = jnp.concatenate([first, second], axis=1).astype(BF16)

    give_mix = across(mix_ref, mixin_ref, mix_send, mix_recv)
    give_back = across(back_ref, backin_ref, back_send, back_recv)
    give_wo = across(wo_ref, wo_ref, wo_send, wo_recv.at[0])

    @pl.when(sec == 0)
    def _():
        inverse = lax.rsqrt(sq_ref[...] / width + EPSILON)
        acc_ref[...] = acc_ref[...] * inverse
        pin_ref[...] = pre_ref[0:t1, 0:rank] * inverse
        _, _, _, probs, mixed = attention()
        mix_ref[...] = mixed
        give_mix.start()
        prb_ref[...] = probs.astype(BF16)
        give_back.wait_recv()
        dmixed = backin_ref[:, 0:hd]
        wide_out = backin_ref[:, hd : hd + rank]
        dvalue = tn(prb_ref[...], dmixed).astype(BF16)
        finish(mix_ref[...], dvalue, wide_out)
        give_mix.wait_send()
        give_x.wait_send()
        give_wo.wait_send()

    @pl.when(sec == 1)
    def _():
        dmixed = accc_ref[...].astype(BF16)
        plain_out = pre_ref[t1:t2, 0:rank]
        give_mix.wait_recv()
        before = mixin_ref[...]
        moved = nn(before, accm_ref[...].astype(BF16))
        tilted = accl_ref[0:t1, 3 * hd : 4 * hd]
        square = moved[:, 3 * hd : 4 * hd] + 2.0 * tilted
        total = sq_ref[...] + jnp.sum(before.astype(F32) * square, axis=1, keepdims=True)
        inverse = lax.rsqrt(jnp.maximum(total, 0.0) / width + EPSILON)
        acc_ref[...] = (accl_ref[0:t1, 0 : 3 * hd] + moved[:, 0 : 3 * hd]) * inverse
        turned = nt(before, accl_ref[t2:t4, 3 * hd : 4 * hd].astype(BF16))
        pin_ref[...] = (pre_ref[0:t1, rank : 2 * rank] + turned[:, rank : 2 * rank]) * inverse
        q, k, v, probs, mixed = attention()
        rounded = probs.astype(BF16)
        dvalue = tn(rounded, dmixed).astype(BF16)
        dprobs = nt(dmixed, v)
        inner = jnp.sum(dprobs * probs, axis=1, keepdims=True)
        dscores = (probs * (dprobs - inner) * scale).astype(BF16)
        dq = nn(dscores, k).astype(BF16)
        dk = tn(dscores, q).astype(BF16)
        dall = jnp.concatenate([dq, dk, dvalue], axis=1)
        share = jnp.sum(dall.astype(F32) * acc_ref[...], axis=1, keepdims=True)
        share = share * inverse * inverse / width
        to_head = inverse * nt(dall, accm_ref[:, 0 : 3 * hd].astype(BF16))
        to_head = to_head - share * (tilted + moved[:, 3 * hd : 4 * hd])
        to_head = to_head + accl_ref[t1:t2, 3 * hd : 4 * hd]
        to_wide = inverse * nt(dall, accl_ref[t2:t3, 0 : 3 * hd].astype(BF16))
        to_wide = to_wide - share * (pre_ref[0:t1, 0:rank] + turned[:, 0:rank])
        to_wide = jnp.where(valid, to_wide + plain_out, 0.0)
        back_ref[:, 0:hd] = to_head.astype(BF16)
        back_ref[:, hd : hd + rank] = to_wide.astype(BF16)
        back_ref[:, hd + rank : 2 * hd] = jnp.zeros((tokens, hd - rank), BF16)
        give_back.start()
        finish(mixed, dvalue, plain_out.astype(BF16))
        give_back.wait_send()

    def spread(i, carry):
        pltpu.make_async_remote_copy(
            src_ref=blk_ref, dst_ref=all_ref.at[me], send_sem=blk_send, recv_sem=blk_recv,
            device_id={"dp": (me + i) % n}, device_id_type=MESH,
        ).start()
        return carry

    lax.fori_loop(1, n, spread, 0)
    all_ref[me] = blk_ref[...]

    def everyone(ref, send, recv):
        return pltpu.make_async_remote_copy(
            src_ref=ref.at[pl.ds(0, n - 1)], dst_ref=ref.at[pl.ds(0, n - 1)],
            send_sem=send, recv_sem=recv, device_id={"dp": nxt}, device_id_type=MESH,
        )

    told = everyone(own_all, own_send, own_recv)
    told.wait_recv()
    pick_ref[...] = jnp.zeros_like(pick_ref)
    shared = everyone(all_ref, blk_send, blk_recv)
    shared.wait_recv()

    def choose(i, seen):
        for e in range(examples):
            named = jnp.where(own_all[i, pl.ds(e, 1), :] == me, 1.0, 0.0)
            piece = all_ref[i, e].astype(F32)
            for slot in range(CAP):
                weight = jnp.where(seen == float(slot), named, 0.0)
                pick_ref[slot] += weight * piece
            seen = seen + named
        return seen

    lax.fori_loop(0, n, choose, jnp.zeros((1, 2 * rank), F32))
    for slot in range(CAP):
        out_ref[slot, 0] = pick_ref[slot, :, 0:rank].astype(BF16)
        out_ref[slot, 1] = pick_ref[slot, :, rank : 2 * rank].astype(BF16)

    told.wait_send()
    shared.wait_send()

    def drain(s, carry):
        for j in range(parts):
            cw(s, j, place).wait_send()
            ccw(s, j, place).wait_send()
            over(s + 1, j, place, mine).wait_send()
        return carry

    lax.fori_loop(0, n - 1, drain, 0)


def shards(
    boundary, w_query, w_key, w_value, w_out, norm_gain, proj_wide, proj_head, lengths, owners
):
    n = lax.axis_size("dp")
    examples, length, width = boundary.shape[1:]
    rows, hd = w_query.shape[1:]
    rank = proj_wide.shape[0]
    tokens = examples * length
    parts = 2 if rows >= 128 else 1
    near = norm_gain
    if rows % 128:
        near = lax.dynamic_slice_in_dim(near, lax.axis_index("dp") * rows, rows, axis=1)
    padded = -(-examples // 8) * 8
    vmem = pl.BlockSpec(memory_space=pltpu.VMEM)
    smem = pl.BlockSpec(memory_space=pltpu.SMEM)
    dma = pltpu.SemaphoreType.DMA
    out = pl.pallas_call(
        functools.partial(kernel, n, examples, length, parts),
        out_shape=jax.ShapeDtypeStruct((CAP, 2, rank, rank), BF16),
        in_specs=[
            smem, smem, vmem, vmem, vmem, vmem, vmem, vmem, vmem, vmem, vmem,
        ],
        out_specs=vmem,
        scratch_shapes=[
            pltpu.VMEM((width, 4 * hd), BF16),
            pltpu.VMEM((width, hd), BF16),
            pltpu.VMEM((2 * tokens + 2 * rank, width), BF16),
            pltpu.VMEM((2 * tokens + 2 * rank, 4 * hd), F32),
            pltpu.VMEM((hd, 4 * hd), F32),
            pltpu.VMEM((tokens, hd), F32),
            pltpu.VMEM((2 * tokens, 2 * rank), F32),
            pltpu.VMEM((tokens, 3 * hd), F32),
            pltpu.VMEM((tokens, 1), F32),
            pltpu.VMEM((tokens, rank), F32),
            pltpu.VMEM((tokens, tokens), BF16),
            pltpu.VMEM((tokens, hd), BF16),
            pltpu.VMEM((tokens, 2 * hd), BF16),
            pltpu.VMEM((tokens, hd), BF16),
            pltpu.VMEM((tokens, 2 * hd), BF16),
            pltpu.VMEM((examples, rank, 2 * rank), BF16),
            pltpu.VMEM((n, examples, rank, 2 * rank), BF16),
            pltpu.VMEM((padded, 2 * rank), jnp.int32),
            pltpu.VMEM((n, padded, 2 * rank), jnp.int32),
            pltpu.VMEM((CAP, rank, 2 * rank), F32),
            dma, dma((n * parts,)), dma((n * parts,)), dma((n * parts,)), dma, dma((n,)),
            dma, dma, dma, dma, dma, dma,
            dma, dma, dma, dma,
        ],
        compiler_params=pltpu.CompilerParams(
            collective_id=0, has_side_effects=True, vmem_limit_bytes=56 * 1024 * 1024
        ),
    )(
        lengths, owners.T, w_query[0], w_key[0], w_value[0], w_out[0], near,
        boundary.reshape(tokens, width), norm_gain, proj_wide, proj_head[0],
    )
    return out[:, None]


def solution(mesh):
    return jax.shard_map(
        shards,
        mesh=mesh,
        in_specs=(
            P("section", ("groups", "dp"), None, None),
            P("section", "dp", None),
            P("section", "dp", None),
            P("section", "dp", None),
            P("section", None, "dp"),
            P("section", None),
            P(),
            P("section", None, None, None),
            P(("groups", "dp")),
            P(("groups", "dp"), None),
        ),
        out_specs=P(("groups", "dp"), "section", None, None, None),
        check_vma=False,
    )
```
